32 devices in a mesh: expert: 4 (over z), tensor: 8 (over y, x, core).
Axes of the slice: x: 2, y: 2, z: 4, core: 2. Of those that a mesh axis runs over, the one named last changes fastest.
Arguments:
- tokens: bfloat16 [512, 6144], P('expert', 'tensor'), may hold values from -6 to 6
- out_grad: bfloat16 [512, 6144], P('expert', 'tensor'), may hold values from -6 to 6
- expert_ids: int32 [512, 2], P('expert'), may hold values from 0 to 3, all different within a row; in each aligned block of 128 rows (0 to 127, 128 to 255, ...) at most 80 rows name the same one
- route_logits: float32 [512, 2], P('expert'), may hold values from -6 to 6
- w_gate: bfloat16 [4, 6144, 8192], P('expert', 'tensor'), may hold values from -0.078125 to 0.078125
- w_up: bfloat16 [4, 6144, 8192], P('expert', 'tensor'), may hold values from -0.078125 to 0.078125
- w_down: bfloat16 [4, 6144, 8192], P('expert', 'tensor'), may hold values from -0.0625 to 0.0625
- gate_scale: float32 [4, 8192], P('expert', 'tensor'), may hold values from 0.5 to 2
- up_scale: float32 [4, 8192], P('expert', 'tensor'), may hold values from 0.5 to 2
- down_scale: float32 [4, 8192], P('expert', 'tensor'), may hold values from 0.5 to 2
Outputs:
- mixed: bfloat16 [512, 6144], P('expert', 'tensor')
- token_grad: bfloat16 [512, 6144], P('expert', 'tensor')
- logit_grad: float32 [512, 2], P('expert')
- gate_grad: bfloat16 [4, 6144, 8192], P('expert', None, 'tensor')
- up_grad: bfloat16 [4, 6144, 8192], P('expert', None, 'tensor')
- down_grad: bfloat16 [4, 6144, 8192], P('expert', None, 'tensor')
The draws below stay inside these ranges and needn't reach their ends.
Inputs may be any that keep to these rules, and one draw needn't show every extreme that they name: `expert_ids`: each token names two different experts; among the 128 tokens of one index of the expert axis, each expert is named by at most 80.
All inputs are finite; a program needn't handle non-finite values.
Results may differ from the reference program's by a relative error of at most 0.025.
Values may be sent and summed in bfloat16 or wider, within the bound.
A program may use at most 256 MiB of HBM per device.

```python
import math
import jax
import jax.numpy as jnp
import numpy as np
from jax import lax

D = 6144
FF = 8192
TOK_GRP = 128
CAP = 80
EXPERTS = 4
TOKENS = 512
N_TENSOR = 8


def levels(rng, shape, split, smallest, top_value):
    loudness, own = 1.0, jax.random.fold_in(rng, 6)
    for position, parts in split:
        draws = jnp.exp(jax.random.uniform(jax.random.fold_in(own, position), (parts,), jnp.float32, smallest / len(split), top_value / len(split)))
        loudness = loudness * jnp.repeat(draws, shape[position] // parts).reshape([-1 if axis == position else 1 for axis in range(len(shape))])
    return loudness


def shared_out(rng, own, number, rows, count, top, reach, lean):
    order = jax.random.permutation(rng, count)
    crowded, common = load_shares(count, rows * top, reach, lean, True), load_shares(count, rows * top, reach, lean, False)
    places = jnp.arange(count)

    def named(tallies, rotation):
        used = int((tallies > 0).sum())
        fixed = max(1, used // 4)
        moved = fixed + (places - fixed + rotation * (used - fixed)) % max(1, count - fixed)
        return jnp.zeros((count,), jnp.int32).at[order[jnp.where(places < fixed, places, moved)]].set(jnp.asarray(tallies, jnp.int32))

    tallies = jnp.where(number % 4 == 0, named(crowded, number // 4), named(common, number - number // 4 - 1))
    mixed = jax.random.permutation(jax.random.fold_in(own, 3), count)
    donor, taker = mixed[0:count // 2 * 2:2], mixed[1:count // 2 * 2:2]
    slack = jnp.minimum(tallies[donor] - 1, reach - tallies[taker]) // 2
    slack = jnp.where((donor == order[0]) | (taker == order[0]) | (tallies[taker] == 0), 0, jnp.maximum(slack, 0))
    moved = jax.random.randint(jax.random.fold_in(own, 4), (count // 2,), 0, 1 << 20) % (slack + 1)
    tallies = tallies.at[donor].add(-moved).at[taker].add(moved)
    members = jnp.searchsorted(jnp.cumsum(tallies), jnp.arange(rows * top), side="right").astype(jnp.int32)
    table = members.reshape(top, rows).T
    table = table[jax.random.permutation(jax.random.fold_in(own, 1), rows)]
    rotation = jax.random.randint(jax.random.fold_in(own, 2), (rows, 1), 0, top)
    return jnp.take_along_axis(table, (jnp.arange(top)[None, :] + rotation) % top, axis=1)


def load_shares(number_of, total, limit, slope, full):
    portions = [(1 << 20) // math.isqrt(rank ** slope) + 1 for rank in range(1, number_of + 1)]
    largest = limit if full else min(limit, max(-(-total // number_of), total * portions[0] // sum(portions)))
    least = 1 if total - largest >= number_of - 1 else 0
    given, spare = [largest] + [least] * (number_of - 1), total - largest - least * (number_of - 1)
    while spare > 0:
        free = [i for i in range(1, number_of) if given[i] < largest] or [i for i in range(1, number_of) if given[i] < limit]
        whole, left = sum([portions[i] for i in free]), spare
        for i in free:
            extra = min(limit - given[i], max(1, left * portions[i] // whole), spare)
            given[i] = given[i] + extra
            spare = spare - extra
    return np.array(given)


def normal_values(key, dims, spread, most, cuts=(), kind=jnp.bfloat16):
    entries = jax.random.normal(key, dims, jnp.float32) * spread
    if len(cuts) > 0:
        entries = levels(key, dims, cuts, -0.22, 0.18) * entries
    return jnp.clip(entries, min=-most, max=most).astype(kind)


def setup_inputs(seed: int = 0) -> dict:
    seeds = jax.random.split(jax.random.key(seed), 11)
    tokens = normal_values(seeds[0], (TOKENS, D), 1.0, 6.0, ((0, 4), (1, 8)))
    out_grad = normal_values(seeds[1], (TOKENS, D), 1.0, 6.0, ((0, 4), (1, 8)))
    expert_ids_keys = jax.random.split(jax.random.fold_in(seeds[2], 1), TOKENS // TOK_GRP)
    expert_ids_turns = jax.random.permutation(jax.random.fold_in(seeds[2], 3), TOKENS // TOK_GRP)
    expert_ids = jax.vmap(lambda own, number: shared_out(jax.random.fold_in(seeds[2], 2), own, number, TOK_GRP, EXPERTS, 2, CAP, 2))(expert_ids_keys, expert_ids_turns).reshape((TOKENS, 2))
    route_logits = normal_values(seeds[3], (TOKENS, 2), 1.5, 6.0, ((0, 4),), jnp.float32)
    w_gate = normal_values(seeds[4], (EXPERTS, D, FF), D ** -0.5, 0.078125, ((0, 4), (1, 8)))
    w_up = normal_values(seeds[5], (EXPERTS, D, FF), D ** -0.5, 0.078125, ((0, 4), (1, 8)))
    w_down = normal_values(seeds[6], (EXPERTS, D, FF), FF ** -0.5, 0.0625, ((0, 4), (1, 8)))
    gate_scale = jnp.clip(jnp.exp(math.log(2.0) - 1.3862944 * jax.random.uniform(seeds[7], (EXPERTS, FF), jnp.float32) ** levels(seeds[7], (EXPERTS, FF), ((0, 4), (1, 8)), -0.2, 0.2)), 0.5, 2.0)
    up_scale = jnp.clip(jnp.exp(math.log(2.0) - 1.3862944 * jax.random.uniform(seeds[8], (EXPERTS, FF), jnp.float32) ** levels(seeds[8], (EXPERTS, FF), ((0, 4), (1, 8)), -0.2, 0.2)), 0.5, 2.0)
    down_scale = jnp.clip(jnp.exp(math.log(2.0) - 1.3862944 * jax.random.uniform(seeds[9], (EXPERTS, FF), jnp.float32) ** levels(seeds[9], (EXPERTS, FF), ((0, 4), (1, 8)), -0.2, 0.2)), 0.5, 2.0)
    return dict(tokens=tokens, out_grad=out_grad, expert_ids=expert_ids, route_logits=route_logits, w_gate=w_gate, w_up=w_up, w_down=w_down, gate_scale=gate_scale, up_scale=up_scale, down_scale=down_scale)


def gate_tables(expert_ids, route_logits, count):
    first = jax.nn.sigmoid(route_logits[:, 0] - route_logits[:, 1])
    probs = jnp.stack([first, 1.0 - first], axis=1)
    labels = jnp.arange(count, dtype=jnp.int32)
    chosen = (expert_ids[:, :, None] == labels[None, None, :]).astype(jnp.float32)
    per_expert = jnp.sum(probs[:, :, None] * chosen, axis=1)
    member = jnp.sum(chosen, axis=1)
    return probs, chosen, per_expert, member


def rounded(value):
    return lax.optimization_barrier(value.astype(jnp.bfloat16)).astype(jnp.float32)


def sliced_sum(lefts, rights):
    rows = lefts[0].shape[0]
    width = FF // N_TENSOR
    left_parts = [left.reshape(rows, N_TENSOR, width).transpose(1, 0, 2) for left in lefts]
    right_parts = [right.reshape(D, N_TENSOR, width).transpose(1, 0, 2) for right in rights]

    def step(total, items):
        part = jnp.zeros((rows, D), jnp.float32)
        for left_one, right_one in zip(items[0], items[1]):
            part = part + jnp.dot(left_one, right_one.T, preferred_element_type=jnp.float32)
        return total + rounded(part), None

    total, _ = lax.scan(step, jnp.zeros((rows, D), jnp.float32), (left_parts, right_parts))
    return total


def contract_rows(left, right):
    return lax.dot_general(left, right, (((0,), (0,)), ((), ())), preferred_element_type=jnp.float32)


def reference(tokens, out_grad, expert_ids, route_logits, w_gate, w_up, w_down, gate_scale, up_scale, down_scale):
    probs, chosen, per_expert, member = gate_tables(expert_ids, route_logits, EXPERTS)
    grad_float = out_grad.astype(jnp.float32)
    mixed_sum = jnp.zeros(tokens.shape, jnp.float32)
    back_sum = jnp.zeros(tokens.shape, jnp.float32)
    scores = []
    gate_grads = []
    up_grads = []
    down_grads = []
    for expert in range(EXPERTS):
        rows_in = tokens * member[:, expert, None].astype(jnp.bfloat16)
        grads_in = (grad_float * per_expert[:, expert, None]).astype(jnp.bfloat16)
        gate_pre = jnp.dot(rows_in, w_gate[expert], preferred_element_type=jnp.float32) * gate_scale[expert]
        up_pre = jnp.dot(rows_in, w_up[expert], preferred_element_type=jnp.float32) * up_scale[expert]
        sigma = jax.nn.sigmoid(gate_pre)
        active = gate_pre * sigma
        hidden = (active * up_pre * down_scale[expert]).astype(jnp.bfloat16)
        expert_out = sliced_sum([hidden], [w_down[expert]]).astype(jnp.bfloat16)
        out_float = expert_out.astype(jnp.float32)
        mixed_sum = mixed_sum + per_expert[:, expert, None] * out_float
        scores.append(jnp.sum(grad_float * out_float, axis=1))
        down_grads.append(contract_rows(grads_in, hidden).astype(jnp.bfloat16))
        back = jnp.dot(grads_in, w_down[expert], preferred_element_type=jnp.float32) * down_scale[expert]
        d_gate = (back * up_pre * sigma * (1.0 + gate_pre * (1.0 - sigma)) * gate_scale[expert]).astype(jnp.bfloat16)
        d_up = (back * active * up_scale[expert]).astype(jnp.bfloat16)
        gate_grads.append(contract_rows(rows_in, d_gate).astype(jnp.bfloat16))
        up_grads.append(contract_rows(rows_in, d_up).astype(jnp.bfloat16))
        tok_back = sliced_sum([d_gate, d_up], [w_gate[expert], w_up[expert]]).astype(jnp.bfloat16)
        back_sum = back_sum + tok_back.astype(jnp.float32)
    score = jnp.stack(scores, axis=1)
    pick = jnp.sum(chosen * score[:, None, :], axis=2)
    mean_pick = jnp.sum(probs * pick, axis=1, keepdims=True)
    logit_grad = probs * (pick - mean_pick)
    return (mixed_sum.astype(jnp.bfloat16), back_sum.astype(jnp.bfloat16), logit_grad,
            jnp.stack(gate_grads), jnp.stack(up_grads), jnp.stack(down_grads))
```

```python
import jax
import jax.numpy as jnp
from jax import lax
from jax.sharding import PartitionSpec as P


def gate_tables(expert_ids, route_logits, count):
    first = jax.nn.sigmoid(route_logits[:, 0] - route_logits[:, 1])
    probs = jnp.stack([first, 1.0 - first], axis=1)
    labels = jnp.arange(count, dtype=jnp.int32)
    chosen = (expert_ids[:, :, None] == labels[None, None, :]).astype(jnp.float32)
    per_expert = jnp.sum(probs[:, :, None] * chosen, axis=1)
    member = jnp.sum(chosen, axis=1)
    return (probs, chosen, per_expert, member)


def contract_rows(left, right):
    return lax.dot_general(
        left, right, (((0,), (0,)), ((), ())), preferred_element_type=jnp.float32
    )


def body(
    tokens,
    out_grad,
    expert_ids,
    route_logits,
    w_gate,
    w_up,
    w_down,
    gate_scale,
    up_scale,
    down_scale,
):
    groups = lax.axis_size("expert")
    local_tokens, feat_width = tokens.shape
    cap = local_tokens * 5 // 8
    total_rows = groups * cap
    probs, chosen, per_expert, member = gate_tables(expert_ids, route_logits, groups)
    weight_cols = per_expert.T[:, :, None]
    earlier = jnp.tril(jnp.ones((local_tokens, local_tokens), jnp.bfloat16), -1)
    rank = jnp.dot(earlier, member.astype(jnp.bfloat16), preferred_element_type=jnp.float32)
    slots = jnp.arange(cap, dtype=jnp.float32)
    place = jnp.where(
        (member.T[:, None, :] > 0) & (rank.T[:, None, :] == slots[None, :, None]), 1.0, 0.0
    ).astype(jnp.bfloat16)

    weighted = (out_grad.astype(jnp.float32)[None] * weight_cols).astype(jnp.bfloat16)
    send_rows = jnp.einsum("eit,td->eid", place, tokens, preferred_element_type=jnp.float32)
    send_grads = jnp.einsum("eit,etd->eid", place, weighted, preferred_element_type=jnp.float32)
    send = jnp.stack([send_rows, send_grads], axis=1).astype(jnp.bfloat16)
    got = lax.all_to_all(send, "expert", split_axis=0, concat_axis=0, tiled=True)
    rows_loc = got[:, 0].reshape(total_rows, feat_width)
    grads_loc = got[:, 1].reshape(total_rows, feat_width)
    gate_w, up_w, down_w = w_gate[0], w_up[0], w_down[0]

    def project(left, right):
        part = jnp.dot(left, right, preferred_element_type=jnp.float32).astype(jnp.bfloat16)
        full = lax.psum_scatter(part, "tensor", scatter_dimension=1, tiled=True)
        return full.astype(jnp.float32)

    def gather(value):
        return lax.all_gather(value, "tensor", axis=1, tiled=True)

    def back_project(left, right):
        return lax.dot_general(
            left, right, (((1,), (1,)), ((), ())), preferred_element_type=jnp.float32
        )

    def send_back(value):
        return lax.all_to_all(
            value.astype(jnp.bfloat16).reshape(groups, cap, feat_width),
            "expert",
            split_axis=0,
            concat_axis=0,
            tiled=True,
        )

    gate_pre = project(rows_loc, gate_w) * gate_scale[0]
    up_pre = project(rows_loc, up_w) * up_scale[0]
    back = project(grads_loc, down_w) * down_scale[0]
    rows_in = gather(rows_loc)
    grads_in = gather(grads_loc)
    sigma = jax.nn.sigmoid(gate_pre)
    active = gate_pre * sigma
    hidden = (active * up_pre * down_scale[0]).astype(jnp.bfloat16)
    d_gate = (back * up_pre * sigma * (1.0 + gate_pre * (1.0 - sigma)) * gate_scale[0]).astype(
        jnp.bfloat16
    )
    d_up = (back * active * up_scale[0]).astype(jnp.bfloat16)
    out_back = send_back(back_project(gather(hidden), down_w))
    grad_back = send_back(
        back_project(gather(d_gate), gate_w) + back_project(gather(d_up), up_w)
    )
    down_grad = contract_rows(grads_in, hidden).astype(jnp.bfloat16)
    gate_grad = contract_rows(rows_in, d_gate).astype(jnp.bfloat16)
    up_grad = contract_rows(rows_in, d_up).astype(jnp.bfloat16)
    out_float = jnp.einsum("eit,eid->etd", place, out_back, preferred_element_type=jnp.float32)
    token_grad = lax.dot_general(
        place.reshape(total_rows, local_tokens),
        grad_back.reshape(total_rows, feat_width),
        (((0,), (0,)), ((), ())),
        preferred_element_type=jnp.float32,
    ).astype(jnp.bfloat16)
    mixed = jnp.sum(weight_cols * out_float, axis=0).astype(jnp.bfloat16)
    local_score = jnp.einsum("td,etd->te", out_grad.astype(jnp.float32), out_float)
    score = lax.psum(local_score, "tensor")
    pick = jnp.sum(chosen * score[:, None, :], axis=2)
    mean_pick = jnp.sum(probs * pick, axis=1, keepdims=True)
    logit_grad = probs * (pick - mean_pick)
    return (mixed, token_grad, logit_grad, gate_grad[None], up_grad[None], down_grad[None])


def solution(mesh):
    in_specs = (
        P("expert", "tensor"),
        P("expert", "tensor"),
        P("expert", None),
        P("expert", None),
        P("expert", "tensor", None),
        P("expert", "tensor", None),
        P("expert", "tensor", None),
        P("expert", "tensor"),
        P("expert", "tensor"),
        P("expert", "tensor"),
    )
    out_specs = (
        P("expert", "tensor"),
        P("expert", "tensor"),
        P("expert", None),
        P("expert", None, "tensor"),
        P("expert", None, "tensor"),
        P("expert", None, "tensor"),
    )
    return jax.shard_map(body, mesh=mesh, in_specs=in_specs, out_specs=out_specs, check_vma=False)
```
